32 devices in a mesh: pix: 4 (over y, x), tm: 8 (over z, core).
Axes of the slice: x: 2, y: 2, z: 4, core: 2. Of those that a mesh axis runs over, the one named last changes fastest.
Arguments:
- movie: bfloat16 [80, 128, 1024], P('pix', None, 'tm'), may hold values from -6 to 6
- noise_weight: float32 [80, 128], P('pix'), may hold values from 0.25 to 4
- footprints: bfloat16 [80, 4, 128, 512], P('pix')
- block_ids: int32 [80, 4], P('pix'), may hold values from 0 to 31, as said below
- band_width: int32 [1024], replicated, may hold values from 0 to 5, as said below
- precision_blocks: bfloat16 [11, 128, 128], replicated
Outputs:
- traces: bfloat16 [16384, 1024], P('pix', 'tm')
- residual: bfloat16 [80, 128, 1024], P('pix', None, 'tm')
The draws below stay inside these ranges and needn't reach their ends.
Inputs may be any that keep to these rules, and one draw needn't show every extreme that they name: `block_ids`: each tile names 4 different component blocks. `band_width`: some group has the reach 5.
All inputs are finite; a program needn't handle non-finite values.
Results may differ from the reference program's by a relative error of at most 0.015.
Values may be sent and summed in bfloat16 or wider, within the bound.
A program may use at most 128 MiB of HBM per device.

```python
import math
import jax
import jax.numpy as jnp
from jax import lax

K = 16384
CBLK = 512
TILE = 128
SLOTS = 4
GROUP = 16
BMAX = 5
FR = 128
TILES = 80
T_SIZE = 1024
KB = 32
NG = 1024
GROUPS_DEV = 32
N_PIX = 4


def draw_footprints(key, part):
    scale_top = (3.0 * KB / (TILE * TILES * SLOTS)) ** 0.5
    shape_all = (TILES, SLOTS, TILE, CBLK)
    key_value, key_keep = jax.random.split(jax.random.fold_in(key, 17))
    values = jax.random.uniform(key_value, shape_all, jnp.float32, 0.0, 1.0)
    kept = jax.random.bernoulli(key_keep, 0.1, shape_all).astype(jnp.float32)
    return (values * kept * 10.0 ** 0.5 * scale_top).astype(jnp.bfloat16)


def draw_block_ids(key, part):
    tile_keys = jax.random.split(key, TILES)

    def one_tile(tile_key):
        return jax.random.permutation(tile_key, KB)[:SLOTS]
    return jax.vmap(one_tile)(tile_keys).astype(jnp.int32)


def draw_band_width(key, part):
    key_base, key_hot, key_forced = jax.random.split(key, 3)
    base_reach = jax.random.randint(key_base, (NG,), 0, 3)
    hot_ranges = jax.random.randint(key_hot, (NG // GROUPS_DEV,), 0, 4) == 0
    hot_groups = jnp.repeat(hot_ranges, GROUPS_DEV)
    widths = jnp.where(hot_groups, BMAX, base_reach)
    forced = jax.random.randint(key_forced, (), 0, NG)
    return widths.at[forced].set(BMAX).astype(jnp.int32)


def draw_precision_blocks(key, part):
    offset_count = 2 * BMAX + 1
    offsets = jnp.abs(jnp.arange(offset_count) - BMAX).astype(jnp.float32)
    decay_scale = (0.7 ** offsets)[:, None, None]
    random_part = jax.random.normal(key, (offset_count, FR, FR), jnp.float32)
    blocks = decay_scale * random_part / FR ** 0.5
    identity = jnp.eye(FR, dtype=jnp.float32)
    center = (offsets == 0).astype(jnp.float32)[:, None, None]
    return (blocks + center * identity).astype(jnp.bfloat16)


def shard_levels(key, dims, cuts, smallest, largest):
    gain = 1.0
    for axis_at, blocks in cuts:
        steps = jax.random.uniform(jax.random.fold_in(jax.random.fold_in(key, 6), axis_at), (blocks,), jnp.float32, smallest / len(cuts), largest / len(cuts))
        gain = gain * jnp.repeat(jnp.exp(steps), dims[axis_at] // blocks).reshape((-1,) + (1,) * (len(dims) - 1 - axis_at))
    return gain


def gaussian(rng, dims, deviation, reach, cuts=(), held_as=jnp.bfloat16):
    level = shard_levels(rng, dims, cuts, -0.22, 0.18) if cuts else 1.0
    entries = jax.random.normal(rng, dims, jnp.float32) * deviation * level
    return jnp.minimum(jnp.maximum(entries, -reach), reach).astype(held_as)


def setup_inputs(seed: int = 0) -> dict:
    keys = jax.random.split(jax.random.key(seed), 7)
    return {
        "movie": gaussian(keys[0], (TILES, TILE, T_SIZE), 1.0, 6.0, ((0, 4), (2, 8))),
        "noise_weight": jnp.clip(jnp.exp(math.log(4.0) - 2.7725887 * jax.random.uniform(keys[1], (TILES, TILE), jnp.float32) ** shard_levels(keys[1], (TILES, TILE), ((0, 4),), -0.2, 0.2)), 0.25, 4.0),
        "footprints": draw_footprints(jax.random.fold_in(keys[6], 71), 0),
        "block_ids": draw_block_ids(jax.random.fold_in(keys[6], 71), 0),
        "band_width": draw_band_width(jax.random.fold_in(keys[6], 71), 0),
        "precision_blocks": draw_precision_blocks(jax.random.fold_in(keys[6], 71), 0),
    }


def reference(movie, noise_weight, footprints, block_ids, band_width, precision_blocks):
    frames = movie.shape[2]
    weighted = (noise_weight[:, :, None] * movie.astype(jnp.float32)).astype(jnp.bfloat16)

    def project(running, item):
        feet, idents, pixels = item
        contrib = jnp.einsum('spc,pf->scf', feet.astype(jnp.float32), pixels.astype(jnp.float32))
        return running.at[idents].add(contrib), None

    def one_index(total, item):
        feet, idents, pixels = item
        start = jnp.zeros((K // CBLK, CBLK, frames), jnp.float32)
        part_sum, _ = lax.scan(project, start, (feet, idents, pixels))
        rounded = lax.optimization_barrier(part_sum.astype(jnp.bfloat16)).astype(jnp.float32)
        return total + rounded, None

    tiles_all = movie.shape[0]
    per_index = tiles_all // N_PIX
    grouped = (footprints.reshape(N_PIX, per_index, SLOTS, TILE, CBLK),
               block_ids.reshape(N_PIX, per_index, SLOTS),
               weighted.reshape(N_PIX, per_index, TILE, frames))
    initial = jnp.zeros((K // CBLK, CBLK, frames), jnp.float32)
    summed, _ = lax.scan(one_index, initial, grouped)
    projected = summed.reshape(K, frames).astype(jnp.bfloat16)
    nblocks = frames // FR
    blocks = projected.astype(jnp.float32).reshape(K, nblocks, FR)
    padded = jnp.pad(blocks, ((0, 0), (BMAX, BMAX), (0, 0)))
    widths = jnp.repeat(band_width, GROUP)
    filtered = jnp.zeros((K, nblocks, FR), jnp.float32)
    for offset in range(-BMAX, BMAX + 1):
        shifted = padded[:, BMAX + offset:BMAX + offset + nblocks, :]
        term = jnp.einsum('kbf,fh->kbh', shifted, precision_blocks[offset + BMAX].astype(jnp.float32))
        inside = (abs(offset) <= widths).astype(jnp.float32)
        filtered = filtered + inside[:, None, None] * term
    traces = filtered.reshape(K, frames).astype(jnp.bfloat16)
    trace_blocks = traces.reshape(K // CBLK, CBLK, frames)

    def rebuild(item):
        feet, idents, pixels = item
        chosen = trace_blocks[idents].astype(jnp.float32)
        rebuilt = jnp.einsum('spc,scf->pf', feet.astype(jnp.float32), chosen)
        return (pixels.astype(jnp.float32) - rebuilt).astype(jnp.bfloat16)

    residual = lax.map(rebuild, (footprints, block_ids, movie))
    return traces, residual
```

```python
import functools

import jax
import jax.numpy as jnp
from jax import lax
from jax.experimental import pallas as pl
from jax.experimental.pallas import tpu as pltpu
from jax.sharding import PartitionSpec as P

K = 16384
CBLK = 512
GROUP = 16
BMAX = 5
FR = 128
LANE = 128
MESH = pl.DeviceIdType.MESH
VMEM_LIMIT = 56 * 1024 * 1024


def project_kernel(ids_ref, movie_ref, noise_ref, feet_ref, out_ref, acc_ref):
    tile = pl.program_id(0)

    @pl.when(tile == 0)
    def _():
        acc_ref[...] = jnp.zeros_like(acc_ref)

    pixels = movie_ref[0].astype(jnp.float32)
    weight = noise_ref[pl.ds(tile, 1), :]
    weighted = (pixels.T * weight).astype(jnp.bfloat16)
    slots = feet_ref.shape[1]
    for slot in range(slots):
        block = ids_ref[tile * slots + slot]
        acc_ref[block] += jnp.dot(
            weighted, feet_ref[0, slot], preferred_element_type=jnp.float32
        )

    @pl.when(tile == pl.num_programs(0) - 1)
    def _():
        def put(b, carry):
            out_ref[b] = acc_ref[b].astype(out_ref.dtype)
            return carry

        lax.fori_loop(0, out_ref.shape[0], put, 0)


def project(movie, noise_weight, footprints, block_ids):
    tiles, slots, pixels, width = footprints.shape
    frames = movie.shape[2]
    blocks = K // CBLK
    return pl.pallas_call(
        project_kernel,
        grid_spec=pltpu.PrefetchScalarGridSpec(
            num_scalar_prefetch=1,
            grid=(tiles,),
            in_specs=[
                pl.BlockSpec((1, pixels, frames), lambda n, ids: (n, 0, 0)),
                pl.BlockSpec((tiles, pixels), lambda n, ids: (0, 0)),
                pl.BlockSpec((1, slots, pixels, width), lambda n, ids: (n, 0, 0, 0)),
            ],
            out_specs=pl.BlockSpec((blocks, frames, width), lambda n, ids: (0, 0, 0)),
            scratch_shapes=[pltpu.VMEM((blocks, frames, width), jnp.float32)],
        ),
        out_shape=jax.ShapeDtypeStruct((blocks, frames, width), jnp.bfloat16),
        compiler_params=pltpu.CompilerParams(vmem_limit_bytes=VMEM_LIMIT),
        name="project",
    )(block_ids.reshape(-1), movie, noise_weight, footprints)


def rebuild_kernel(ids_ref, movie_ref, feet_ref, traces_ref, out_ref):
    tile = pl.program_id(0)
    slots = feet_ref.shape[1]
    total = movie_ref[0].astype(jnp.float32)
    for slot in range(slots):
        block = ids_ref[tile * slots + slot]
        total = total - jnp.dot(
            feet_ref[0, slot], traces_ref[block], preferred_element_type=jnp.float32
        )
    out_ref[0] = total.astype(out_ref.dtype)


def rebuild(movie, footprints, block_ids, traces):
    tiles, slots, pixels, width = footprints.shape
    frames = movie.shape[2]
    blocks = K // CBLK
    return pl.pallas_call(
        rebuild_kernel,
        grid_spec=pltpu.PrefetchScalarGridSpec(
            num_scalar_prefetch=1,
            grid=(tiles,),
            in_specs=[
                pl.BlockSpec((1, pixels, frames), lambda n, ids: (n, 0, 0)),
                pl.BlockSpec((1, slots, pixels, width), lambda n, ids: (n, 0, 0, 0)),
                pl.BlockSpec((blocks, width, frames), lambda n, ids: (0, 0, 0)),
            ],
            out_specs=pl.BlockSpec((1, pixels, frames), lambda n, ids: (n, 0, 0)),
        ),
        out_shape=jax.ShapeDtypeStruct(movie.shape, jnp.bfloat16),
        compiler_params=pltpu.CompilerParams(vmem_limit_bytes=VMEM_LIMIT),
        name="rebuild",
    )(block_ids.reshape(-1), movie, footprints, traces.reshape(blocks, width, frames))


def middle_kernel(
    n_pix, n_tm, part_ref, reach_ref, prec_ref, out_ref,
    rs_buf, x_buf, xt_buf, y_buf,
    rs_s, rs_r, a_s, a_r, b_s, b_r, g_s, g_r,
):
    chunks = rs_buf.shape[0]
    blocks_chunk = rs_buf.shape[2]
    lanes = xt_buf.shape[3]
    groups = CBLK // lanes
    blocks_pix = chunks * blocks_chunk
    me_p = lax.axis_index("pix")
    me_t = lax.axis_index("tm")

    def pix_at(e):
        return lax.rem(me_p + e, n_pix)

    def tm_at(e):
        return lax.rem(me_t + e, n_tm)

    barrier = pltpu.get_barrier_semaphore()
    for e in range(1, n_pix):
        pl.semaphore_signal(
            barrier, inc=1, device_id={"pix": pix_at(e)}, device_id_type=MESH
        )
    for e in range(1, n_tm):
        pl.semaphore_signal(
            barrier, inc=1, device_id={"tm": tm_at(e)}, device_id_type=MESH
        )
    pl.semaphore_wait(barrier, n_pix + n_tm - 2)

    def rs_copy(c, e):
        peer = pix_at(e)
        return pltpu.make_async_remote_copy(
            src_ref=part_ref.at[pl.ds(peer * blocks_pix + c * blocks_chunk, blocks_chunk)],
            dst_ref=rs_buf.at[c, e - 1],
            send_sem=rs_s.at[c, e - 1],
            recv_sem=rs_r.at[c, e - 1],
            device_id={"pix": peer},
            device_id_type=MESH,
        )

    def a_copy(c, e):
        peer = tm_at(e)
        return pltpu.make_async_remote_copy(
            src_ref=x_buf.at[c, peer],
            dst_ref=xt_buf.at[c, me_t + BMAX],
            send_sem=a_s.at[c, e - 1],
            recv_sem=a_r.at[c, e - 1],
            device_id={"tm": peer},
            device_id_type=MESH,
        )

    def b_copy(c, e):
        peer = tm_at(e)
        return pltpu.make_async_remote_copy(
            src_ref=y_buf.at[c, peer],
            dst_ref=out_ref.at[me_p, c, me_t],
            send_sem=b_s.at[c, e - 1],
            recv_sem=b_r.at[c, e - 1],
            device_id={"tm": peer},
            device_id_type=MESH,
        )

    def g_copy(c, e):
        peer = pix_at(e)
        return pltpu.make_async_remote_copy(
            src_ref=out_ref.at[me_p, c],
            dst_ref=out_ref.at[me_p, c],
            send_sem=g_s.at[c, e - 1],
            recv_sem=g_r.at[c, e - 1],
            device_id={"pix": peer},
            device_id_type=MESH,
        )

    for c in range(chunks):
        for e in range(1, n_pix):
            rs_copy(c, e).start()

    edge = jnp.zeros((BMAX,) + xt_buf.shape[2:], xt_buf.dtype)
    for c in range(chunks):
        xt_buf[c, pl.ds(0, BMAX)] = edge
        xt_buf[c, pl.ds(BMAX + n_tm, BMAX)] = edge

    def sum_chunk(c):
        for e in range(1, n_pix):
            rs_copy(c, e).wait_recv()
        for part in range(n_tm):
            b, g = part // groups, part % groups
            span = slice(g * lanes, (g + 1) * lanes)
            total = part_ref[me_p * blocks_pix + c * blocks_chunk + b, :, span].astype(jnp.float32)
            for e in range(1, n_pix):
                total = total + rs_buf[c, e - 1, b, :, span].astype(jnp.float32)
            x_buf[c, part] = total.astype(x_buf.dtype)
        for e in range(1, n_tm):
            a_copy(c, e).start()
        xt_buf[c, me_t + BMAX] = x_buf[c, me_t]

    def filter_chunk(c):
        for e in range(1, n_tm):
            a_copy(c, e).wait_recv()
        reach = reach_ref[pl.ds(c, 1), :]
        keep = [
            jnp.where(reach >= k, 1.0, 0.0).astype(jnp.bfloat16) for k in range(BMAX + 1)
        ]

        def one_block(i):
            source = jnp.concatenate(
                [xt_buf[c, i + d + BMAX] * keep[abs(d)] for d in range(-BMAX, BMAX + 1)],
                axis=0,
            )
            result = jnp.dot(prec_ref[...], source, preferred_element_type=jnp.float32)
            return result.T.astype(jnp.bfloat16)

        def step(e, carry):
            peer = tm_at(e)
            y_buf[c, peer] = one_block(peer)
            return carry

        lax.fori_loop(0, n_tm, step, 0)
        for e in range(1, n_tm):
            b_copy(c, e).start()
        out_ref[me_p, c, me_t] = y_buf[c, me_t]

    def gather_chunk(c):
        for e in range(1, n_tm):
            b_copy(c, e).wait_recv()
        for e in range(1, n_pix):
            g_copy(c, e).start()

    for t in range(chunks + 2):
        if t < chunks:
            sum_chunk(t)
        if 0 <= t - 1 < chunks:
            filter_chunk(t - 1)
        if 0 <= t - 2:
            gather_chunk(t - 2)

    for c in range(chunks):
        for e in range(1, n_pix):
            g_copy(c, e).wait_recv()
    for c in range(chunks):
        for e in range(1, n_pix):
            rs_copy(c, e).wait_send()
            g_copy(c, e).wait_send()
        for e in range(1, n_tm):
            a_copy(c, e).wait_send()
            b_copy(c, e).wait_send()


def middle(partial_value, band_width, precision_blocks):
    blocks, frames, width = partial_value.shape
    n_pix, n_tm = lax.axis_size("pix"), lax.axis_size("tm")
    chunks = K // (n_pix * n_tm * LANE)
    blocks_chunk = blocks // (n_pix * chunks)
    reach = jnp.repeat(band_width, GROUP).reshape(n_pix, chunks, n_tm, LANE)
    reach = lax.dynamic_index_in_dim(reach, lax.axis_index("pix"), 0, keepdims=False)
    reach = lax.dynamic_index_in_dim(reach, lax.axis_index("tm"), 1, keepdims=False)
    stacked = precision_blocks.reshape(-1, FR).T
    dma = pltpu.SemaphoreType.DMA
    bf16 = jnp.bfloat16
    vmem = pl.BlockSpec(memory_space=pltpu.VMEM)
    gathered = pl.pallas_call(
        functools.partial(middle_kernel, n_pix, n_tm),
        out_shape=jax.ShapeDtypeStruct((n_pix, chunks, n_tm, LANE, frames), bf16),
        in_specs=[vmem, vmem, vmem],
        out_specs=vmem,
        scratch_shapes=[
            pltpu.VMEM((chunks, n_pix - 1, blocks_chunk, frames, width), bf16),
            pltpu.VMEM((chunks, n_tm, frames, LANE), bf16),
            pltpu.VMEM((chunks, n_tm + 2 * BMAX, frames, LANE), bf16),
            pltpu.VMEM((chunks, n_tm, LANE, frames), bf16),
            dma((chunks, n_pix - 1)), dma((chunks, n_pix - 1)),
            dma((chunks, n_tm - 1)), dma((chunks, n_tm - 1)),
            dma((chunks, n_tm - 1)), dma((chunks, n_tm - 1)),
            dma((chunks, n_pix - 1)), dma((chunks, n_pix - 1)),
        ],
        compiler_params=pltpu.CompilerParams(
            collective_id=0, has_side_effects=True, vmem_limit_bytes=VMEM_LIMIT
        ),
        name="middle",
    )(partial_value, reach, stacked)
    traces = lax.dynamic_index_in_dim(gathered, lax.axis_index("pix"), 0, keepdims=False)
    return gathered.reshape(K, frames), traces.reshape(K // n_pix, frames)


def middle_plain(partial_value, band_width, precision_blocks):
    blocks, frames, width = partial_value.shape
    n_pix, n_tm = lax.axis_size("pix"), lax.axis_size("tm")
    summed = lax.psum_scatter(partial_value, "pix", scatter_dimension=0, tiled=True)
    rows = summed.transpose(0, 2, 1).reshape(K // n_pix, frames)
    moved = lax.all_to_all(rows, "tm", split_axis=0, concat_axis=1, tiled=True)
    here = moved.shape[0]
    start = (lax.axis_index("pix") * n_tm + lax.axis_index("tm")) * here
    widths = lax.dynamic_slice_in_dim(jnp.repeat(band_width, GROUP), start, here)
    nblocks = moved.shape[1] // FR
    padded = jnp.pad(moved.reshape(here, nblocks, FR), ((0, 0), (BMAX, BMAX), (0, 0)))
    filtered = jnp.zeros((here, nblocks, FR), jnp.float32)
    for d in range(2 * BMAX + 1):
        term = jnp.einsum(
            "kbf,fh->kbh", padded[:, d:d + nblocks], precision_blocks[d],
            preferred_element_type=jnp.float32,
        )
        filtered = filtered + jnp.where((abs(d - BMAX) <= widths)[:, None, None], term, 0.0)
    local = filtered.reshape(here, nblocks * FR).astype(jnp.bfloat16)
    traces = lax.all_to_all(local, "tm", split_axis=1, concat_axis=0, tiled=True)
    return lax.all_gather(traces, "pix", axis=0, tiled=True), traces


def shards(movie, noise_weight, footprints, block_ids, band_width, precision_blocks):
    n_pix, n_tm = lax.axis_size("pix"), lax.axis_size("tm")
    partial_value = project(movie, noise_weight, footprints, block_ids)
    fits = movie.shape[2] == FR and K % (n_pix * n_tm * LANE) == 0
    fits = fits and (K // CBLK) % (n_pix * (K // (n_pix * n_tm * LANE))) == 0
    form = middle if fits else middle_plain
    all_traces, traces = form(partial_value, band_width, precision_blocks)
    residual = rebuild(movie, footprints, block_ids, all_traces)
    return (traces, residual)


def solution(mesh):
    return jax.shard_map(
        shards,
        mesh=mesh,
        in_specs=(
            P("pix", None, "tm"),
            P("pix", None),
            P("pix", None, None, None),
            P("pix", None),
            P(),
            P(),
        ),
        out_specs=(P("pix", "tm"), P("pix", None, "tm")),
        check_vma=False,
    )
```

```python
import functools

import jax
import jax.numpy as jnp
from jax import lax
from jax.experimental import pallas as pl
from jax.experimental.pallas import tpu as pltpu
from jax.sharding import PartitionSpec as P

K = 16384
CBLK = 512
GROUP = 16
BMAX = 5
FR = 128
LANE = 128
SIDE = 2
HALVES = 2
MESH = pl.DeviceIdType.MESH
VMEM_LIMIT = 56 * 1024 * 1024


def tile_batch(tiles):
    return 4 if tiles % 4 == 0 else 1


def project_kernel(ids_ref, movie_ref, noise_ref, feet_ref, out_ref, acc_ref):
    tile = pl.program_id(0)

    @pl.when(tile == 0)
    def _():
        acc_ref[...] = jnp.zeros_like(acc_ref)

    batch, slots = feet_ref.shape[:2]
    for member in range(batch):
        at = tile * batch + member
        pixels = movie_ref[member].astype(jnp.float32)
        weighted = (pixels.T * noise_ref[pl.ds(at, 1), :]).astype(jnp.bfloat16)
        products = [
            jnp.dot(weighted, feet_ref[member, slot], preferred_element_type=jnp.float32)
            for slot in range(slots)
        ]
        for slot in range(slots):
            acc_ref[ids_ref[at * slots + slot]] += products[slot]

    @pl.when(tile == pl.num_programs(0) - 1)
    def _():
        def put(b, carry):
            out_ref[b] = acc_ref[b].astype(out_ref.dtype)
            return carry

        lax.fori_loop(0, out_ref.shape[0], put, 0)


def project(movie, noise_weight, footprints, block_ids):
    tiles, slots, pixels, width = footprints.shape
    frames = movie.shape[2]
    blocks = K // CBLK
    batch = tile_batch(tiles)
    return pl.pallas_call(
        project_kernel,
        grid_spec=pltpu.PrefetchScalarGridSpec(
            num_scalar_prefetch=1,
            grid=(tiles // batch,),
            in_specs=[
                pl.BlockSpec((batch, pixels, frames), lambda n, ids: (n, 0, 0)),
                pl.BlockSpec((tiles, pixels), lambda n, ids: (0, 0)),
                pl.BlockSpec((batch, slots, pixels, width), lambda n, ids: (n, 0, 0, 0)),
            ],
            out_specs=pl.BlockSpec((blocks, frames, width), lambda n, ids: (0, 0, 0)),
            scratch_shapes=[pltpu.VMEM((blocks, frames, width), jnp.float32)],
        ),
        out_shape=jax.ShapeDtypeStruct((blocks, frames, width), jnp.bfloat16),
        compiler_params=pltpu.CompilerParams(vmem_limit_bytes=VMEM_LIMIT),
        name="project",
    )(block_ids.reshape(-1), movie, noise_weight, footprints)


def rebuild_kernel(ids_ref, me_ref, movie_ref, feet_ref, traces_ref, own_ref, out_ref):
    tile = pl.program_id(0)

    @pl.when(tile == 0)
    def _():
        count = own_ref.shape[0]

        def put(b, carry):
            own_ref[b] = traces_ref[me_ref[0] * count + b]
            return carry

        lax.fori_loop(0, count, put, 0)

    batch, slots = feet_ref.shape[:2]
    for member in range(batch):
        at = tile * batch + member
        rebuilt = None
        for slot in range(slots):
            term = jnp.dot(
                feet_ref[member, slot], traces_ref[ids_ref[at * slots + slot]],
                preferred_element_type=jnp.float32,
            )
            rebuilt = term if rebuilt is None else rebuilt + term
        out_ref[member] = (movie_ref[member].astype(jnp.float32) - rebuilt).astype(out_ref.dtype)


def rebuild(movie, footprints, block_ids, traces):
    tiles, slots, pixels, width = footprints.shape
    frames = movie.shape[2]
    blocks = K // CBLK
    n_pix = lax.axis_size("pix")
    batch = tile_batch(tiles)
    own = (blocks // n_pix, width, frames)
    own_traces, residual = pl.pallas_call(
        rebuild_kernel,
        grid_spec=pltpu.PrefetchScalarGridSpec(
            num_scalar_prefetch=2,
            grid=(tiles // batch,),
            in_specs=[
                pl.BlockSpec((batch, pixels, frames), lambda n, ids, me: (n, 0, 0)),
                pl.BlockSpec((batch, slots, pixels, width), lambda n, ids, me: (n, 0, 0, 0)),
                pl.BlockSpec((blocks, width, frames), lambda n, ids, me: (0, 0, 0)),
            ],
            out_specs=[
                pl.BlockSpec(own, lambda n, ids, me: (0, 0, 0)),
                pl.BlockSpec((batch, pixels, frames), lambda n, ids, me: (n, 0, 0)),
            ],
        ),
        out_shape=[
            jax.ShapeDtypeStruct(own, jnp.bfloat16),
            jax.ShapeDtypeStruct(movie.shape, jnp.bfloat16),
        ],
        compiler_params=pltpu.CompilerParams(vmem_limit_bytes=VMEM_LIMIT),
        name="rebuild",
    )(
        block_ids.reshape(-1), lax.axis_index("pix").reshape(1),
        movie, footprints, traces.reshape(blocks, width, frames),
    )
    return own_traces.reshape(K // n_pix, frames), residual


def middle_kernel(
    n_pix, n_tm, part_ref, reach_ref, prec_ref, out_ref,
    far_buf, near_buf, hop_out, hop_in, x_buf, xt_buf, y_buf,
    far_s, far_r, near_s, near_r, hop_s, hop_r,
    a_s, a_r, b_s, b_r, g_s, g_r, relay_s, relay_r,
):
    chunks = far_buf.shape[0]
    lanes = xt_buf.shape[3]
    groups = CBLK // lanes
    parts_half = n_tm // HALVES
    me_p = lax.axis_index("pix")
    me_t = lax.axis_index("tm")
    me_x = lax.rem(me_p, SIDE)
    along_x = me_p + 1 - 2 * me_x
    along_y = lax.rem(me_p + SIDE, n_pix)
    across = lax.rem(along_x + SIDE, n_pix)
    first = (along_x, along_y)
    second = (along_y, along_x)

    def tm_at(e):
        return lax.rem(me_t + e, n_tm)

    def part_at(owner, c, h):
        return (owner * chunks + c) * HALVES + h

    barrier = pltpu.get_barrier_semaphore()
    for peer in first:
        pl.semaphore_signal(barrier, inc=1, device_id={"pix": peer}, device_id_type=MESH)
    for e in range(1, n_tm):
        pl.semaphore_signal(
            barrier, inc=1, device_id={"tm": tm_at(e)}, device_id_type=MESH
        )
    pl.semaphore_wait(barrier, len(first) + n_tm - 1)

    def pix_copy(source, target, send, recv, c, h, peer):
        return pltpu.make_async_remote_copy(
            src_ref=source, dst_ref=target, send_sem=send.at[c, h], recv_sem=recv.at[c, h],
            device_id={"pix": peer}, device_id_type=MESH,
        )

    def far_copy(c, h):
        source = part_ref.at[part_at(across, c, h)]
        return pix_copy(source, far_buf.at[c, h], far_s, far_r, c, h, first[h])

    def near_copy(c, h):
        source = part_ref.at[part_at(first[h], c, h)]
        return pix_copy(source, near_buf.at[c, h], near_s, near_r, c, h, first[h])

    def hop_copy(c, h):
        return pix_copy(hop_out.at[c, h], hop_in.at[c, h], hop_s, hop_r, c, h, second[h])

    def g_copy(c, h):
        rows = out_ref.at[me_p, c]
        return pix_copy(rows, rows, g_s, g_r, c, h, first[h])

    def relay_copy(c, h):
        rows = out_ref.at[first[h], c, pl.ds(h * parts_half, parts_half)]
        return pix_copy(rows, rows, relay_s, relay_r, c, h, second[h])

    def a_copy(c, e):
        peer = tm_at(e)
        return pltpu.make_async_remote_copy(
            src_ref=x_buf.at[c, peer],
            dst_ref=xt_buf.at[c, me_t + BMAX],
            send_sem=a_s.at[c, e - 1],
            recv_sem=a_r.at[c, e - 1],
            device_id={"tm": peer},
            device_id_type=MESH,
        )

    def b_copy(c, e):
        peer = tm_at(e)
        return pltpu.make_async_remote_copy(
            src_ref=y_buf.at[c, peer],
            dst_ref=out_ref.at[me_p, c, me_t],
            send_sem=b_s.at[c, e - 1],
            recv_sem=b_r.at[c, e - 1],
            device_id={"tm": peer},
            device_id_type=MESH,
        )

    def send_far(c):
        for h in range(HALVES):
            far_copy(c, h).start()

    def send_near(c):
        for h in range(HALVES):
            near_copy(c, h).start()

    def send_hop(c):
        for h in range(HALVES):
            far_copy(c, h).wait_recv()
            total = part_ref[part_at(second[h], c, h)].astype(jnp.float32)
            total = total + far_buf[c, h].astype(jnp.float32)
            hop_out[c, h] = total.astype(hop_out.dtype)
            hop_copy(c, h).start()

    def sum_chunk(c):
        for h in range(HALVES):
            near_copy(c, h).wait_recv()
            hop_copy(c, h).wait_recv()
            for g in range(groups):
                span = slice(g * lanes, (g + 1) * lanes)
                total = part_ref[part_at(me_p, c, h), :, span].astype(jnp.float32)
                total = total + near_buf[c, h, :, span].astype(jnp.float32)
                total = total + hop_in[c, h, :, span].astype(jnp.float32)
                x_buf[c, h * groups + g] = total.astype(x_buf.dtype)
        for e in range(1, n_tm):
            a_copy(c, e).start()
        xt_buf[c, me_t + BMAX] = x_buf[c, me_t]

    def filter_chunk(c):
        for e in range(1, n_tm):
            a_copy(c, e).wait_recv()
        reach = reach_ref[pl.ds(c, 1), :]
        keep = [
            jnp.where(reach >= k, 1.0, 0.0).astype(jnp.bfloat16) for k in range(BMAX + 1)
        ]

        def one_block(i):
            source = jnp.concatenate(
                [xt_buf[c, i + d + BMAX] * keep[abs(d)] for d in range(-BMAX, BMAX + 1)],
                axis=0,
            )
            result = jnp.dot(prec_ref[...], source, preferred_element_type=jnp.float32)
            return result.T.astype(jnp.bfloat16)

        def step(e, carry):
            peer = tm_at(e)
            y_buf[c, peer] = one_block(peer)
            return carry

        lax.fori_loop(0, n_tm, step, 0)
        for e in range(1, n_tm):
            b_copy(c, e).start()
        out_ref[me_p, c, me_t] = y_buf[c, me_t]

    def gather_chunk(c):
        for e in range(1, n_tm):
            b_copy(c, e).wait_recv()
        for h in range(HALVES):
            g_copy(c, h).start()

    def relay_chunk(c):
        for h in range(HALVES):
            g_copy(c, h).wait_recv()
            relay_copy(c, h).start()

    send_far(0)
    send_near(0)
    edge = jnp.zeros((BMAX,) + xt_buf.shape[2:], xt_buf.dtype)
    for c in range(chunks):
        xt_buf[c, pl.ds(0, BMAX)] = edge
        xt_buf[c, pl.ds(BMAX + n_tm, BMAX)] = edge
    if chunks > 1:
        send_far(1)
    for t in range(chunks + 3):
        if t < chunks:
            send_hop(t)
        if t + 1 < chunks:
            send_near(t + 1)
        if t + 2 < chunks:
            send_far(t + 2)
        if t < chunks:
            sum_chunk(t)
        if 0 <= t - 1 < chunks:
            filter_chunk(t - 1)
        if 0 <= t - 2 < chunks:
            gather_chunk(t - 2)
        if 0 <= t - 3:
            relay_chunk(t - 3)

    for c in range(chunks):
        for h in range(HALVES):
            relay_copy(c, h).wait_recv()
    for c in range(chunks):
        for h in range(HALVES):
            for copy in (far_copy, near_copy, hop_copy, g_copy, relay_copy):
                copy(c, h).wait_send()
        for e in range(1, n_tm):
            a_copy(c, e).wait_send()
            b_copy(c, e).wait_send()


def middle(partial_value, band_width, precision_blocks):
    blocks, frames, width = partial_value.shape
    n_pix, n_tm = lax.axis_size("pix"), lax.axis_size("tm")
    chunks = K // (n_pix * n_tm * LANE)
    reach = jnp.repeat(band_width, GROUP).reshape(n_pix, chunks, n_tm, LANE)
    reach = lax.dynamic_index_in_dim(reach, lax.axis_index("pix"), 0, keepdims=False)
    reach = lax.dynamic_index_in_dim(reach, lax.axis_index("tm"), 1, keepdims=False)
    stacked = precision_blocks.reshape(-1, FR).T
    dma = pltpu.SemaphoreType.DMA
    bf16 = jnp.bfloat16
    vmem = pl.BlockSpec(memory_space=pltpu.VMEM)
    gathered = pl.pallas_call(
        functools.partial(middle_kernel, n_pix, n_tm),
        out_shape=jax.ShapeDtypeStruct((n_pix, chunks, n_tm, LANE, frames), bf16),
        in_specs=[vmem, vmem, vmem],
        out_specs=vmem,
        scratch_shapes=[pltpu.VMEM((chunks, HALVES, frames, width), bf16)] * 4 + [
            pltpu.VMEM((chunks, n_tm, frames, LANE), bf16),
            pltpu.VMEM((chunks, n_tm + 2 * BMAX, frames, LANE), bf16),
            pltpu.VMEM((chunks, n_tm, LANE, frames), bf16),
        ] + [dma((chunks, HALVES))] * 6 + [dma((chunks, n_tm - 1))] * 4
        + [dma((chunks, HALVES))] * 4,
        compiler_params=pltpu.CompilerParams(
            collective_id=0, has_side_effects=True, vmem_limit_bytes=VMEM_LIMIT
        ),
        name="middle",
    )(partial_value, reach, stacked)
    return gathered.reshape(K, frames)


def middle_plain(partial_value, band_width, precision_blocks):
    blocks, frames, width = partial_value.shape
    n_pix, n_tm = lax.axis_size("pix"), lax.axis_size("tm")
    summed = lax.psum_scatter(partial_value, "pix", scatter_dimension=0, tiled=True)
    rows = summed.transpose(0, 2, 1).reshape(K // n_pix, frames)
    moved = lax.all_to_all(rows, "tm", split_axis=0, concat_axis=1, tiled=True)
    here = moved.shape[0]
    start = (lax.axis_index("pix") * n_tm + lax.axis_index("tm")) * here
    widths = lax.dynamic_slice_in_dim(jnp.repeat(band_width, GROUP), start, here)
    nblocks = moved.shape[1] // FR
    padded = jnp.pad(moved.reshape(here, nblocks, FR), ((0, 0), (BMAX, BMAX), (0, 0)))
    filtered = jnp.zeros((here, nblocks, FR), jnp.float32)
    for d in range(2 * BMAX + 1):
        term = jnp.einsum(
            "kbf,fh->kbh", padded[:, d:d + nblocks], precision_blocks[d],
            preferred_element_type=jnp.float32,
        )
        filtered = filtered + jnp.where((abs(d - BMAX) <= widths)[:, None, None], term, 0.0)
    local = filtered.reshape(here, nblocks * FR).astype(jnp.bfloat16)
    traces = lax.all_to_all(local, "tm", split_axis=1, concat_axis=0, tiled=True)
    return lax.all_gather(traces, "pix", axis=0, tiled=True)


def shards(movie, noise_weight, footprints, block_ids, band_width, precision_blocks):
    n_pix, n_tm = lax.axis_size("pix"), lax.axis_size("tm")
    partial_value = project(movie, noise_weight, footprints, block_ids)
    fits = movie.shape[2] == FR and K % (n_pix * n_tm * LANE) == 0
    fits = fits and n_pix == SIDE * SIDE and n_tm * LANE == HALVES * CBLK
    form = middle if fits else middle_plain
    all_traces = form(partial_value, band_width, precision_blocks)
    return rebuild(movie, footprints, block_ids, all_traces)


def solution(mesh):
    return jax.shard_map(
        shards,
        mesh=mesh,
        in_specs=(
            P("pix", None, "tm"),
            P("pix", None),
            P("pix", None, None, None),
            P("pix", None),
            P(),
            P(),
        ),
        out_specs=(P("pix", "tm"), P("pix", None, "tm")),
        check_vma=False,
    )
```

```python
import functools

import jax
import jax.numpy as jnp
from jax import lax
from jax.experimental import pallas as pl
from jax.experimental.pallas import tpu as pltpu
from jax.sharding import PartitionSpec as P

K = 16384
CBLK = 512
GROUP = 16
BMAX = 5
FR = 128
LANE = 128
SIDE = 2
HALVES = 2
MESH = pl.DeviceIdType.MESH
VMEM_LIMIT = 56 * 1024 * 1024


def tile_batch(tiles):
    return 4 if tiles % 4 == 0 else 1


def project_kernel(ids_ref, movie_ref, noise_ref, feet_ref, out_ref, acc_ref):
    tile = pl.program_id(0)

    @pl.when(tile == 0)
    def _():
        acc_ref[...] = jnp.zeros_like(acc_ref)

    batch, slots = feet_ref.shape[:2]
    for member in range(batch):
        at = tile * batch + member
        pixels = movie_ref[member].astype(jnp.float32)
        weighted = (pixels.T * noise_ref[pl.ds(at, 1), :]).astype(jnp.bfloat16)
        products = [
            jnp.dot(weighted, feet_ref[member, slot], preferred_element_type=jnp.float32)
            for slot in range(slots)
        ]
        for slot in range(slots):
            acc_ref[ids_ref[at, slot]] += products[slot]

    @pl.when(tile == pl.num_programs(0) - 1)
    def _():
        def put(b, carry):
            for c in range(out_ref.shape[0]):
                span = slice(c * LANE, (c + 1) * LANE)
                out_ref[c, b] = acc_ref[b, :, span].astype(out_ref.dtype)
            return carry

        lax.fori_loop(0, out_ref.shape[1], put, 0)


def project(movie, noise_weight, footprints, block_ids):
    tiles, slots, pixels, width = footprints.shape
    frames = movie.shape[2]
    blocks = K // CBLK
    batch = tile_batch(tiles)
    shape = (width // LANE, blocks, frames, LANE)
    return pl.pallas_call(
        project_kernel,
        grid_spec=pltpu.PrefetchScalarGridSpec(
            num_scalar_prefetch=1,
            grid=(tiles // batch,),
            in_specs=[
                pl.BlockSpec((batch, pixels, frames), lambda n, ids: (n, 0, 0)),
                pl.BlockSpec((tiles, pixels), lambda n, ids: (0, 0)),
                pl.BlockSpec((batch, slots, pixels, width), lambda n, ids: (n, 0, 0, 0)),
            ],
            out_specs=pl.BlockSpec(shape, lambda n, ids: (0, 0, 0, 0)),
            scratch_shapes=[pltpu.VMEM((blocks, frames, width), jnp.float32)],
        ),
        out_shape=jax.ShapeDtypeStruct(shape, jnp.bfloat16),
        compiler_params=pltpu.CompilerParams(vmem_limit_bytes=VMEM_LIMIT),
        name="project",
    )(block_ids, movie, noise_weight, footprints)


def rebuild_kernel(ids_ref, me_ref, movie_ref, feet_ref, traces_ref, own_ref, out_ref):
    tile = pl.program_id(0)

    @pl.when(tile == 0)
    def _():
        count = own_ref.shape[0]

        def put(b, carry):
            own_ref[b] = traces_ref[me_ref[0] * count + b]
            return carry

        lax.fori_loop(0, count, put, 0)

    batch, slots = feet_ref.shape[:2]
    for member in range(batch):
        at = tile * batch + member
        rebuilt = None
        for slot in range(slots):
            term = jnp.dot(
                feet_ref[member, slot], traces_ref[ids_ref[at, slot]],
                preferred_element_type=jnp.float32,
            )
            rebuilt = term if rebuilt is None else rebuilt + term
        out_ref[member] = (movie_ref[member].astype(jnp.float32) - rebuilt).astype(out_ref.dtype)


def rebuild(movie, footprints, block_ids, traces):
    tiles, slots, pixels, width = footprints.shape
    frames = movie.shape[2]
    blocks = K // CBLK
    n_pix = lax.axis_size("pix")
    batch = tile_batch(tiles)
    own = (blocks // n_pix, width, frames)
    own_traces, residual = pl.pallas_call(
        rebuild_kernel,
        grid_spec=pltpu.PrefetchScalarGridSpec(
            num_scalar_prefetch=2,
            grid=(tiles // batch,),
            in_specs=[
                pl.BlockSpec((batch, pixels, frames), lambda n, ids, me: (n, 0, 0)),
                pl.BlockSpec((batch, slots, pixels, width), lambda n, ids, me: (n, 0, 0, 0)),
                pl.BlockSpec((blocks, width, frames), lambda n, ids, me: (0, 0, 0)),
            ],
            out_specs=[
                pl.BlockSpec(own, lambda n, ids, me: (0, 0, 0)),
                pl.BlockSpec((batch, pixels, frames), lambda n, ids, me: (n, 0, 0)),
            ],
        ),
        out_shape=[
            jax.ShapeDtypeStruct(own, jnp.bfloat16),
            jax.ShapeDtypeStruct(movie.shape, jnp.bfloat16),
        ],
        compiler_params=pltpu.CompilerParams(vmem_limit_bytes=VMEM_LIMIT),
        name="rebuild",
    )(
        block_ids, lax.axis_index("pix").reshape(1),
        movie, footprints, traces.reshape(blocks, width, frames),
    )
    return own_traces.reshape(K // n_pix, frames), residual


def middle_kernel(
    n_pix, n_tm, ids_ref, part_ref, reach_ref, prec_ref, movie_ref, feet_hbm,
    traces_ref, residual_ref,
    far_buf, near_buf, hop_out, hop_in, x_buf, xt_buf, y_buf,
    prec_t, feet_ref, total_ref,
    far_s, far_r, near_s, near_r, hop_s, hop_r,
    g_s, g_r, relay_s, relay_r, a_s, a_r, b_s, b_r, feet_sem, *gathered,
):
    chunks = far_buf.shape[0]
    parts_half = n_tm // HALVES
    me_p = lax.axis_index("pix")
    me_t = lax.axis_index("tm")
    me_x = lax.rem(me_p, SIDE)
    along_x = me_p + 1 - 2 * me_x
    along_y = lax.rem(me_p + SIDE, n_pix)
    across = lax.rem(along_x + SIDE, n_pix)
    first = (along_x, along_y)
    second = (along_y, along_x)

    def tm_at(e):
        return lax.rem(me_t + e, n_tm)

    def part_at(owner, h):
        return pl.ds(owner * n_tm + h * parts_half, parts_half)

    load_feet = pltpu.make_async_copy(feet_hbm, feet_ref, feet_sem)

    barrier = pltpu.get_barrier_semaphore()
    for peer in first:
        pl.semaphore_signal(barrier, inc=1, device_id={"pix": peer}, device_id_type=MESH)
    for e in range(1, n_tm):
        pl.semaphore_signal(
            barrier, inc=1, device_id={"tm": tm_at(e)}, device_id_type=MESH
        )
    pl.semaphore_wait(barrier, len(first) + n_tm - 1)

    def pix_copy(source, target, send, recv, c, h, peer):
        return pltpu.make_async_remote_copy(
            src_ref=source, dst_ref=target, send_sem=send.at[c, h], recv_sem=recv.at[c, h],
            device_id={"pix": peer}, device_id_type=MESH,
        )

    def far_copy(c, h):
        source = part_ref.at[c, part_at(across, h)]
        return pix_copy(source, far_buf.at[c, h], far_s, far_r, c, h, first[h])

    def near_copy(c, h):
        source = part_ref.at[c, part_at(first[h], h)]
        return pix_copy(source, near_buf.at[c, h], near_s, near_r, c, h, first[h])

    def hop_copy(c, h):
        return pix_copy(hop_out.at[c, h], hop_in.at[c, h], hop_s, hop_r, c, h, second[h])

    def g_copy(c, h):
        rows = gathered[c].at[pl.ds(me_p * n_tm, n_tm)]
        return pix_copy(rows, rows, g_s, g_r, c, h, first[h])

    def relay_copy(c, h):
        rows = gathered[c].at[part_at(first[h], h)]
        return pix_copy(rows, rows, relay_s, relay_r, c, h, second[h])

    def a_copy(c, e):
        peer = tm_at(e)
        return pltpu.make_async_remote_copy(
            src_ref=x_buf.at[c, peer],
            dst_ref=xt_buf.at[c, me_t + BMAX],
            send_sem=a_s.at[c, e - 1],
            recv_sem=a_r.at[c, e - 1],
            device_id={"tm": peer},
            device_id_type=MESH,
        )

    def b_copy(c, e):
        peer = tm_at(e)
        return pltpu.make_async_remote_copy(
            src_ref=y_buf.at[c, peer],
            dst_ref=gathered[c].at[me_p * n_tm + me_t],
            send_sem=b_s.at[c, e - 1],
            recv_sem=b_r.at[c, e - 1],
            device_id={"tm": peer},
            device_id_type=MESH,
        )

    def send_far(c):
        for h in range(HALVES):
            far_copy(c, h).start()

    def send_near(c):
        for h in range(HALVES):
            near_copy(c, h).start()

    def send_hop(c):
        for h in range(HALVES):
            far_copy(c, h).wait_recv()
            for g in range(parts_half):
                total = part_ref[c, second[h] * n_tm + h * parts_half + g].astype(jnp.float32)
                total = total + far_buf[c, h, g].astype(jnp.float32)
                hop_out[c, h, g] = total.astype(hop_out.dtype)
            hop_copy(c, h).start()

    def sum_chunk(c):
        for h in range(HALVES):
            near_copy(c, h).wait_recv()
            hop_copy(c, h).wait_recv()
            for g in range(parts_half):
                part = h * parts_half + g
                total = part_ref[c, me_p * n_tm + part].astype(jnp.float32)
                total = total + near_buf[c, h, g].astype(jnp.float32)
                total = total + hop_in[c, h, g].astype(jnp.float32)
                x_buf[c, part] = total.astype(x_buf.dtype)
        for e in range(1, n_tm):
            a_copy(c, e).start()
        xt_buf[c, me_t + BMAX] = x_buf[c, me_t]

    def filter_chunk(c):
        for e in range(1, n_tm):
            a_copy(c, e).wait_recv()
        reach = reach_ref[pl.ds(c, 1), :]
        keep = [
            jnp.where(reach >= k, 1.0, 0.0).astype(jnp.bfloat16) for k in range(BMAX + 1)
        ]

        def one_block(i):
            source = jnp.concatenate(
                [xt_buf[c, i + d + BMAX] * keep[abs(d)] for d in range(-BMAX, BMAX + 1)],
                axis=0,
            )
            result = jnp.dot(prec_t[...], source, preferred_element_type=jnp.float32)
            return result.T.astype(jnp.bfloat16)

        def step(e, carry):
            peer = tm_at(e)
            y_buf[c, peer] = one_block(peer)
            return carry

        lax.fori_loop(0, n_tm, step, 0)
        for e in range(1, n_tm):
            b_copy(c, e).start()
        gathered[c][me_p * n_tm + me_t] = y_buf[c, me_t]

    def gather_chunk(c):
        for e in range(1, n_tm):
            b_copy(c, e).wait_recv()
        for h in range(HALVES):
            g_copy(c, h).start()
        for j in range(n_tm):
            traces_ref[j, c * LANE:(c + 1) * LANE, :] = gathered[c][me_p * n_tm + j]

    def relay_chunk(c):
        for h in range(HALVES):
            g_copy(c, h).wait_recv()
            relay_copy(c, h).start()

    def rebuild_chunk(c):
        for h in range(HALVES):
            relay_copy(c, h).wait_recv()
        if c == 0:
            load_feet.wait()
        tiles, slots = feet_ref.shape[:2]
        span = slice(c * LANE, (c + 1) * LANE)

        def one_tile(n):
            feet = jnp.concatenate([feet_ref[n, slot, :, span] for slot in range(slots)], axis=1)
            chosen = jnp.concatenate(
                [gathered[c][ids_ref[n, slot]] for slot in range(slots)], axis=0
            )
            rebuilt = jnp.dot(feet, chosen, preferred_element_type=jnp.float32)
            if c > 0:
                rebuilt = rebuilt + total_ref[n]
            if c < chunks - 1:
                total_ref[n] = rebuilt
            else:
                left = movie_ref[n].astype(jnp.float32) - rebuilt
                residual_ref[n] = left.astype(residual_ref.dtype)

        batch = tile_batch(tiles)

        def step(k, carry):
            for member in range(batch):
                one_tile(k * batch + member)
            return carry

        lax.fori_loop(0, tiles // batch, step, 0)

    send_far(0)
    send_near(0)
    load_feet.start()
    for d in range(prec_ref.shape[0]):
        matrix = prec_ref[d].astype(jnp.float32)
        prec_t[:, d * FR:(d + 1) * FR] = matrix.T.astype(prec_t.dtype)
    edge = jnp.zeros((BMAX,) + xt_buf.shape[2:], xt_buf.dtype)
    for c in range(chunks):
        xt_buf[c, pl.ds(0, BMAX)] = edge
        xt_buf[c, pl.ds(BMAX + n_tm, BMAX)] = edge
    if chunks > 1:
        send_far(1)
    for t in range(chunks + 4):
        if t < chunks:
            send_hop(t)
        if t + 1 < chunks:
            send_near(t + 1)
        if t + 2 < chunks:
            send_far(t + 2)
        if t < chunks:
            sum_chunk(t)
        if 0 <= t - 1 < chunks:
            filter_chunk(t - 1)
        if 0 <= t - 2 < chunks:
            gather_chunk(t - 2)
        if 0 <= t - 3 < chunks:
            relay_chunk(t - 3)
        if 0 <= t - 4:
            rebuild_chunk(t - 4)

    for c in range(chunks):
        for h in range(HALVES):
            for copy in (far_copy, near_copy, hop_copy, g_copy, relay_copy):
                copy(c, h).wait_send()
        for e in range(1, n_tm):
            a_copy(c, e).wait_send()
            b_copy(c, e).wait_send()


def middle(partial_value, movie, footprints, block_ids, band_width, precision_blocks):
    chunks, blocks, frames, lanes = partial_value.shape
    n_pix, n_tm = lax.axis_size("pix"), lax.axis_size("tm")
    reach = jnp.repeat(band_width.reshape(blocks, chunks, -1), GROUP, axis=2)
    mine = lax.axis_index("pix") * n_tm + lax.axis_index("tm")
    reach = lax.dynamic_index_in_dim(reach, mine, 0, keepdims=False)
    dma = pltpu.SemaphoreType.DMA
    bf16 = jnp.bfloat16
    vmem = pl.BlockSpec(memory_space=pltpu.VMEM)
    part = (frames, lanes)
    traces, residual = pl.pallas_call(
        functools.partial(middle_kernel, n_pix, n_tm),
        out_shape=[
            jax.ShapeDtypeStruct((n_tm, CBLK, frames), bf16),
            jax.ShapeDtypeStruct(movie.shape, bf16),
        ],
        in_specs=[pl.BlockSpec(memory_space=pltpu.SMEM)] + [vmem] * 4
        + [pl.BlockSpec(memory_space=pl.ANY)],
        out_specs=[vmem, vmem],
        scratch_shapes=[pltpu.VMEM((chunks, HALVES, n_tm // HALVES) + part, bf16)] * 4 + [
            pltpu.VMEM((chunks, n_tm) + part, bf16),
            pltpu.VMEM((chunks, n_tm + 2 * BMAX) + part, bf16),
            pltpu.VMEM((chunks, n_tm, lanes, frames), bf16),
            pltpu.VMEM((FR, precision_blocks.shape[0] * FR), bf16),
            pltpu.VMEM(footprints.shape, bf16),
            pltpu.VMEM(movie.shape, jnp.float32),
        ] + [dma((chunks, HALVES))] * 10 + [dma((chunks, n_tm - 1))] * 4 + [dma]
        + [pltpu.VMEM((blocks, lanes, frames), bf16)] * chunks,
        compiler_params=pltpu.CompilerParams(
            collective_id=0, has_side_effects=True, vmem_limit_bytes=VMEM_LIMIT
        ),
        name="middle",
    )(block_ids, partial_value, reach, precision_blocks, movie, footprints)
    return traces.reshape(K // n_pix, frames), residual


def middle_plain(partial_value, movie, footprints, block_ids, band_width, precision_blocks):
    frames = movie.shape[2]
    n_pix, n_tm = lax.axis_size("pix"), lax.axis_size("tm")
    summed = lax.psum_scatter(partial_value, "pix", scatter_dimension=1, tiled=True)
    rows = summed.transpose(1, 0, 3, 2).reshape(K // n_pix, frames)
    moved = lax.all_to_all(rows, "tm", split_axis=0, concat_axis=1, tiled=True)
    here = moved.shape[0]
    start = (lax.axis_index("pix") * n_tm + lax.axis_index("tm")) * here
    widths = lax.dynamic_slice_in_dim(jnp.repeat(band_width, GROUP), start, here)
    nblocks = moved.shape[1] // FR
    padded = jnp.pad(moved.reshape(here, nblocks, FR), ((0, 0), (BMAX, BMAX), (0, 0)))
    filtered = jnp.zeros((here, nblocks, FR), jnp.float32)
    for d in range(2 * BMAX + 1):
        term = jnp.einsum(
            "kbf,fh->kbh", padded[:, d:d + nblocks], precision_blocks[d],
            preferred_element_type=jnp.float32,
        )
        filtered = filtered + jnp.where((abs(d - BMAX) <= widths)[:, None, None], term, 0.0)
    local = filtered.reshape(here, nblocks * FR).astype(jnp.bfloat16)
    traces = lax.all_to_all(local, "tm", split_axis=1, concat_axis=0, tiled=True)
    gathered = lax.all_gather(traces, "pix", axis=0, tiled=True)
    return rebuild(movie, footprints, block_ids, gathered)


def shards(movie, noise_weight, footprints, block_ids, band_width, precision_blocks):
    n_pix, n_tm = lax.axis_size("pix"), lax.axis_size("tm")
    partial_value = project(movie, noise_weight, footprints, block_ids)
    fits = movie.shape[2] == FR and n_pix == SIDE * SIDE and n_pix * n_tm == K // CBLK
    form = middle if fits else middle_plain
    return form(partial_value, movie, footprints, block_ids, band_width, precision_blocks)


def solution(mesh):
    return jax.shard_map(
        shards,
        mesh=mesh,
        in_specs=(
            P("pix", None, "tm"),
            P("pix", None),
            P("pix", None, None, None),
            P("pix", None),
            P(),
            P(),
        ),
        out_specs=(P("pix", "tm"), P("pix", None, "tm")),
        check_vma=False,
    )
```

```python
import functools

import jax
import jax.numpy as jnp
from jax import lax
from jax.experimental import pallas as pl
from jax.experimental.pallas import tpu as pltpu
from jax.sharding import PartitionSpec as P

K = 16384
CBLK = 512
GROUP = 16
BMAX = 5
FR = 128
LANE = 128
SIDE = 2
HALVES = 2
MESH = pl.DeviceIdType.MESH
VMEM_LIMIT = 56 * 1024 * 1024


def tile_batch(tiles):
    return 4 if tiles % 4 == 0 else 1


def project_kernel(ids_ref, movie_ref, noise_ref, feet_ref, out_ref, acc_ref):
    tile = pl.program_id(0)

    @pl.when(tile == 0)
    def _():
        acc_ref[...] = jnp.zeros_like(acc_ref)

    batch, slots = feet_ref.shape[:2]
    for member in range(batch):
        at = tile * batch + member
        pixels = movie_ref[member].astype(jnp.float32)
        weighted = (pixels.T * noise_ref[pl.ds(at, 1), :]).astype(jnp.bfloat16)
        products = [
            jnp.dot(weighted, feet_ref[member, slot], preferred_element_type=jnp.float32)
            for slot in range(slots)
        ]
        for slot in range(slots):
            acc_ref[ids_ref[at, slot]] += products[slot]

    @pl.when(tile == pl.num_programs(0) - 1)
    def _():
        def put(b, carry):
            for c in range(out_ref.shape[0]):
                span = slice(c * LANE, (c + 1) * LANE)
                out_ref[c, b] = acc_ref[b, :, span].astype(out_ref.dtype)
            return carry

        lax.fori_loop(0, out_ref.shape[1], put, 0)


def project(movie, noise_weight, footprints, block_ids):
    tiles, slots, pixels, width = footprints.shape
    frames = movie.shape[2]
    blocks = K // CBLK
    batch = tile_batch(tiles)
    shape = (width // LANE, blocks, frames, LANE)
    return pl.pallas_call(
        project_kernel,
        grid_spec=pltpu.PrefetchScalarGridSpec(
            num_scalar_prefetch=1,
            grid=(tiles // batch,),
            in_specs=[
                pl.BlockSpec((batch, pixels, frames), lambda n, ids: (n, 0, 0)),
                pl.BlockSpec((tiles, pixels), lambda n, ids: (0, 0)),
                pl.BlockSpec((batch, slots, pixels, width), lambda n, ids: (n, 0, 0, 0)),
            ],
            out_specs=pl.BlockSpec(shape, lambda n, ids: (0, 0, 0, 0)),
            scratch_shapes=[pltpu.VMEM((blocks, frames, width), jnp.float32)],
        ),
        out_shape=jax.ShapeDtypeStruct(shape, jnp.bfloat16),
        compiler_params=pltpu.CompilerParams(vmem_limit_bytes=VMEM_LIMIT),
        name="project",
    )(block_ids, movie, noise_weight, footprints)


def rebuild_kernel(ids_ref, me_ref, movie_ref, feet_ref, traces_ref, own_ref, out_ref):
    tile = pl.program_id(0)

    @pl.when(tile == 0)
    def _():
        count = own_ref.shape[0]

        def put(b, carry):
            own_ref[b] = traces_ref[me_ref[0] * count + b]
            return carry

        lax.fori_loop(0, count, put, 0)

    batch, slots = feet_ref.shape[:2]
    for member in range(batch):
        at = tile * batch + member
        rebuilt = None
        for slot in range(slots):
            term = jnp.dot(
                feet_ref[member, slot], traces_ref[ids_ref[at, slot]],
                preferred_element_type=jnp.float32,
            )
            rebuilt = term if rebuilt is None else rebuilt + term
        out_ref[member] = (movie_ref[member].astype(jnp.float32) - rebuilt).astype(out_ref.dtype)


def rebuild(movie, footprints, block_ids, traces):
    tiles, slots, pixels, width = footprints.shape
    frames = movie.shape[2]
    blocks = K // CBLK
    n_pix = lax.axis_size("pix")
    batch = tile_batch(tiles)
    own = (blocks // n_pix, width, frames)
    own_traces, residual = pl.pallas_call(
        rebuild_kernel,
        grid_spec=pltpu.PrefetchScalarGridSpec(
            num_scalar_prefetch=2,
            grid=(tiles // batch,),
            in_specs=[
                pl.BlockSpec((batch, pixels, frames), lambda n, ids, me: (n, 0, 0)),
                pl.BlockSpec((batch, slots, pixels, width), lambda n, ids, me: (n, 0, 0, 0)),
                pl.BlockSpec((blocks, width, frames), lambda n, ids, me: (0, 0, 0)),
            ],
            out_specs=[
                pl.BlockSpec(own, lambda n, ids, me: (0, 0, 0)),
                pl.BlockSpec((batch, pixels, frames), lambda n, ids, me: (n, 0, 0)),
            ],
        ),
        out_shape=[
            jax.ShapeDtypeStruct(own, jnp.bfloat16),
            jax.ShapeDtypeStruct(movie.shape, jnp.bfloat16),
        ],
        compiler_params=pltpu.CompilerParams(vmem_limit_bytes=VMEM_LIMIT),
        name="rebuild",
    )(
        block_ids, lax.axis_index("pix").reshape(1),
        movie, footprints, traces.reshape(blocks, width, frames),
    )
    return own_traces.reshape(K // n_pix, frames), residual


def middle_kernel(
    n_pix, n_tm, ids_ref, part_ref, reach_ref, prec_ref, movie_ref, feet_hbm,
    traces_ref, residual_ref,
    far_buf, near_buf, hop_out, hop_in, x_buf, xt_buf, y_buf,
    prec_t, feet_ref, total_ref,
    far_s, far_r, near_s, near_r, hop_s, hop_r,
    g_s, g_r, relay_s, relay_r, a_s, a_r, b_s, b_r, feet_sem, *gathered,
):
    chunks = far_buf.shape[0]
    parts_half = n_tm // HALVES
    me_p = lax.axis_index("pix")
    me_t = lax.axis_index("tm")
    me_x = lax.rem(me_p, SIDE)
    along_x = me_p + 1 - 2 * me_x
    along_y = lax.rem(me_p + SIDE, n_pix)
    across = lax.rem(along_x + SIDE, n_pix)
    first = (along_x, along_y)
    second = (along_y, along_x)

    def tm_at(e):
        return lax.rem(me_t + e, n_tm)

    def part_at(owner, h):
        return pl.ds(owner * n_tm + h * parts_half, parts_half)

    load_feet = pltpu.make_async_copy(feet_hbm, feet_ref, feet_sem)

    barrier = pltpu.get_barrier_semaphore()
    for peer in first:
        pl.semaphore_signal(barrier, inc=1, device_id={"pix": peer}, device_id_type=MESH)
    for e in range(1, n_tm):
        pl.semaphore_signal(
            barrier, inc=1, device_id={"tm": tm_at(e)}, device_id_type=MESH
        )
    pl.semaphore_wait(barrier, len(first) + n_tm - 1)

    def pix_copy(source, target, send, recv, c, h, peer):
        return pltpu.make_async_remote_copy(
            src_ref=source, dst_ref=target, send_sem=send.at[c, h], recv_sem=recv.at[c, h],
            device_id={"pix": peer}, device_id_type=MESH,
        )

    def far_copy(c, h):
        source = part_ref.at[c, part_at(across, h)]
        return pix_copy(source, far_buf.at[c, h], far_s, far_r, c, h, first[h])

    def near_copy(c, h):
        source = part_ref.at[c, part_at(first[h], h)]
        return pix_copy(source, near_buf.at[c, h], near_s, near_r, c, h, first[h])

    def hop_copy(c, h):
        return pix_copy(hop_out.at[c, h], hop_in.at[c, h], hop_s, hop_r, c, h, second[h])

    def g_copy(c, h):
        rows = gathered[c].at[pl.ds(me_p * n_tm, n_tm)]
        return pix_copy(rows, rows, g_s, g_r, c, h, first[h])

    def relay_copy(c, h):
        rows = gathered[c].at[part_at(first[h], h)]
        return pix_copy(rows, rows, relay_s, relay_r, c, h, second[h])

    def a_copy(c, e):
        peer = tm_at(e)
        return pltpu.make_async_remote_copy(
            src_ref=x_buf.at[c, peer],
            dst_ref=xt_buf.at[c, me_t + BMAX],
            send_sem=a_s.at[c, e - 1],
            recv_sem=a_r.at[c, e - 1],
            device_id={"tm": peer},
            device_id_type=MESH,
        )

    def b_copy(c, e):
        peer = tm_at(e)
        return pltpu.make_async_remote_copy(
            src_ref=y_buf.at[c, peer],
            dst_ref=gathered[c].at[me_p * n_tm + me_t],
            send_sem=b_s.at[c, e - 1],
            recv_sem=b_r.at[c, e - 1],
            device_id={"tm": peer},
            device_id_type=MESH,
        )

    def send_far(c):
        for h in range(HALVES):
            far_copy(c, h).start()

    def send_near(c):
        for h in range(HALVES):
            near_copy(c, h).start()

    def send_hop(c):
        for h in range(HALVES):
            far_copy(c, h).wait_recv()
            for g in range(parts_half):
                total = part_ref[c, second[h] * n_tm + h * parts_half + g].astype(jnp.float32)
                total = total + far_buf[c, h, g].astype(jnp.float32)
                hop_out[c, h, g] = total.astype(hop_out.dtype)
            hop_copy(c, h).start()

    def sum_chunk(c):
        for h in range(HALVES):
            near_copy(c, h).wait_recv()
            hop_copy(c, h).wait_recv()
            for g in range(parts_half):
                part = h * parts_half + g
                total = part_ref[c, me_p * n_tm + part].astype(jnp.float32)
                total = total + near_buf[c, h, g].astype(jnp.float32)
                total = total + hop_in[c, h, g].astype(jnp.float32)
                x_buf[c, part] = total.astype(x_buf.dtype)
        for e in range(1, n_tm):
            a_copy(c, e).start()
        xt_buf[c, me_t + BMAX] = x_buf[c, me_t]

    def filter_chunk(c):
        for e in range(1, n_tm):
            a_copy(c, e).wait_recv()
        reach = reach_ref[pl.ds(c, 1), :]
        keep = [
            jnp.where(reach >= k, 1.0, 0.0).astype(jnp.bfloat16) for k in range(BMAX + 1)
        ]

        def one_block(i):
            source = jnp.concatenate(
                [xt_buf[c, i + d + BMAX] * keep[abs(d)] for d in range(-BMAX, BMAX + 1)],
                axis=0,
            )
            result = jnp.dot(prec_t[...], source, preferred_element_type=jnp.float32)
            return result.T.astype(jnp.bfloat16)

        def step(e, carry):
            peer = tm_at(e)
            y_buf[c, peer] = one_block(peer)
            return carry

        lax.fori_loop(0, n_tm, step, 0)
        for e in range(1, n_tm):
            b_copy(c, e).start()
        gathered[c][me_p * n_tm + me_t] = y_buf[c, me_t]

    def gather_chunk(c):
        for e in range(1, n_tm):
            b_copy(c, e).wait_recv()
        for h in range(HALVES):
            g_copy(c, h).start()
        for j in range(n_tm):
            traces_ref[j, c * LANE:(c + 1) * LANE, :] = gathered[c][me_p * n_tm + j]

    def relay_chunk(c):
        for h in range(HALVES):
            g_copy(c, h).wait_recv()
            relay_copy(c, h).start()

    def rebuild_chunk(c):
        for h in range(HALVES):
            relay_copy(c, h).wait_recv()
        if c == 0:
            load_feet.wait()
        tiles, slots = feet_ref.shape[:2]
        span = slice(c * LANE, (c + 1) * LANE)

        def one_tile(n):
            feet = jnp.concatenate([feet_ref[n, slot, :, span] for slot in range(slots)], axis=1)
            chosen = jnp.concatenate(
                [gathered[c][ids_ref[n, slot]] for slot in range(slots)], axis=0
            )
            rebuilt = jnp.dot(feet, chosen, preferred_element_type=jnp.float32)
            if c > 0:
                rebuilt = rebuilt + total_ref[n]
            if c < chunks - 1:
                total_ref[n] = rebuilt
            else:
                left = movie_ref[n].astype(jnp.float32) - rebuilt
                residual_ref[n] = left.astype(residual_ref.dtype)

        batch = tile_batch(tiles)

        def step(k, carry):
            for member in range(batch):
                one_tile(k * batch + member)
            return carry

        lax.fori_loop(0, tiles // batch, step, 0)

    send_far(0)
    send_near(0)
    load_feet.start()
    for d in range(prec_ref.shape[0]):
        matrix = prec_ref[d].astype(jnp.float32)
        prec_t[:, d * FR:(d + 1) * FR] = matrix.T.astype(prec_t.dtype)
    edge = jnp.zeros((BMAX,) + xt_buf.shape[2:], xt_buf.dtype)
    for c in range(chunks):
        xt_buf[c, pl.ds(0, BMAX)] = edge
        xt_buf[c, pl.ds(BMAX + n_tm, BMAX)] = edge
    if chunks > 1:
        send_far(1)
    for t in range(chunks + 4):
        if t < chunks:
            send_hop(t)
        if t + 1 < chunks:
            send_near(t + 1)
        if t + 2 < chunks:
            send_far(t + 2)
        if t < chunks:
            sum_chunk(t)
            if t >= 2:
                gather_chunk(t - 2)
            if t >= 3:
                relay_chunk(t - 3)
        if 0 <= t - 1 < chunks:
            filter_chunk(t - 1)
        if t >= chunks and 0 <= t - 2 < chunks:
            gather_chunk(t - 2)
        if t >= chunks and 0 <= t - 3 < chunks:
            relay_chunk(t - 3)
        if 0 <= t - 4:
            rebuild_chunk(t - 4)

    for c in range(chunks):
        for h in range(HALVES):
            for copy in (far_copy, near_copy, hop_copy, g_copy, relay_copy):
                copy(c, h).wait_send()
        for e in range(1, n_tm):
            a_copy(c, e).wait_send()
            b_copy(c, e).wait_send()


def middle(partial_value, movie, footprints, block_ids, band_width, precision_blocks):
    chunks, blocks, frames, lanes = partial_value.shape
    n_pix, n_tm = lax.axis_size("pix"), lax.axis_size("tm")
    reach = jnp.repeat(band_width.reshape(blocks, chunks, -1), GROUP, axis=2)
    mine = lax.axis_index("pix") * n_tm + lax.axis_index("tm")
    reach = lax.dynamic_index_in_dim(reach, mine, 0, keepdims=False)
    dma = pltpu.SemaphoreType.DMA
    bf16 = jnp.bfloat16
    vmem = pl.BlockSpec(memory_space=pltpu.VMEM)
    part = (frames, lanes)
    traces, residual = pl.pallas_call(
        functools.partial(middle_kernel, n_pix, n_tm),
        out_shape=[
            jax.ShapeDtypeStruct((n_tm, CBLK, frames), bf16),
            jax.ShapeDtypeStruct(movie.shape, bf16),
        ],
        in_specs=[pl.BlockSpec(memory_space=pltpu.SMEM)] + [vmem] * 4
        + [pl.BlockSpec(memory_space=pl.ANY)],
        out_specs=[vmem, vmem],
        scratch_shapes=[pltpu.VMEM((chunks, HALVES, n_tm // HALVES) + part, bf16)] * 4 + [
            pltpu.VMEM((chunks, n_tm) + part, bf16),
            pltpu.VMEM((chunks, n_tm + 2 * BMAX) + part, bf16),
            pltpu.VMEM((chunks, n_tm, lanes, frames), bf16),
            pltpu.VMEM((FR, precision_blocks.shape[0] * FR), bf16),
            pltpu.VMEM(footprints.shape, bf16),
            pltpu.VMEM(movie.shape, jnp.float32),
        ] + [dma((chunks, HALVES))] * 10 + [dma((chunks, n_tm - 1))] * 4 + [dma]
        + [pltpu.VMEM((blocks, lanes, frames), bf16)] * chunks,
        compiler_params=pltpu.CompilerParams(
            collective_id=0, has_side_effects=True, vmem_limit_bytes=VMEM_LIMIT
        ),
        name="middle",
    )(block_ids, partial_value, reach, precision_blocks, movie, footprints)
    return traces.reshape(K // n_pix, frames), residual


def middle_plain(partial_value, movie, footprints, block_ids, band_width, precision_blocks):
    frames = movie.shape[2]
    n_pix, n_tm = lax.axis_size("pix"), lax.axis_size("tm")
    summed = lax.psum_scatter(partial_value, "pix", scatter_dimension=1, tiled=True)
    rows = summed.transpose(1, 0, 3, 2).reshape(K // n_pix, frames)
    moved = lax.all_to_all(rows, "tm", split_axis=0, concat_axis=1, tiled=True)
    here = moved.shape[0]
    start = (lax.axis_index("pix") * n_tm + lax.axis_index("tm")) * here
    widths = lax.dynamic_slice_in_dim(jnp.repeat(band_width, GROUP), start, here)
    nblocks = moved.shape[1] // FR
    padded = jnp.pad(moved.reshape(here, nblocks, FR), ((0, 0), (BMAX, BMAX), (0, 0)))
    filtered = jnp.zeros((here, nblocks, FR), jnp.float32)
    for d in range(2 * BMAX + 1):
        term = jnp.einsum(
            "kbf,fh->kbh", padded[:, d:d + nblocks], precision_blocks[d],
            preferred_element_type=jnp.float32,
        )
        filtered = filtered + jnp.where((abs(d - BMAX) <= widths)[:, None, None], term, 0.0)
    local = filtered.reshape(here, nblocks * FR).astype(jnp.bfloat16)
    traces = lax.all_to_all(local, "tm", split_axis=1, concat_axis=0, tiled=True)
    gathered = lax.all_gather(traces, "pix", axis=0, tiled=True)
    return rebuild(movie, footprints, block_ids, gathered)


def shards(movie, noise_weight, footprints, block_ids, band_width, precision_blocks):
    n_pix, n_tm = lax.axis_size("pix"), lax.axis_size("tm")
    partial_value = project(movie, noise_weight, footprints, block_ids)
    fits = movie.shape[2] == FR and n_pix == SIDE * SIDE and n_pix * n_tm == K // CBLK
    form = middle if fits else middle_plain
    return form(partial_value, movie, footprints, block_ids, band_width, precision_blocks)


def solution(mesh):
    return jax.shard_map(
        shards,
        mesh=mesh,
        in_specs=(
            P("pix", None, "tm"),
            P("pix", None),
            P("pix", None, None, None),
            P("pix", None),
            P(),
            P(),
        ),
        out_specs=(P("pix", "tm"), P("pix", None, "tm")),
        check_vma=False,
    )
```
